128 devices in a mesh: band: 8 (over x, y_hi), lon: 16 (over z, y_lo, core).
Axes of the slice: x: 4, y: 4 (y_hi: 2, y_lo: 2; y = y_hi * 2 + y_lo), z: 4, core: 2. Of those that a mesh axis runs over, the one named last changes fastest.
Arguments:
- ocean_flux: bfloat16 [2048, 8, 128], P(('band', 'lon')), may hold values from -6 to 6
- remap_weight: bfloat16 [4096, 128, 128], P(('band', 'lon')), may hold values from -0.5 to 0.5
- dest_owner: int32 [12288, 1], P(('band', 'lon')), may hold values from 0 to 127; in each aligned block of 96 rows (0 to 95, 96 to 191, ...) at most 2 rows name the same one
- src_tile: int32 [12288], P(('band', 'lon')), may hold values from 0 to 15
- weight_block: int32 [12288], P(('band', 'lon')), may hold values from 0 to 31
- dest_window: int32 [12288], P(('band', 'lon')), may hold values from 0 to 6
- atmos_state: bfloat16 [16, 7168, 2560], P('band', 'lon'), may hold values from -6 to 6
- profile: float32 [16, 897], P('band'), may hold values from 0.3 to 3
- filter_len: int32 [16], P('band'), may hold values from 449 to 896, as said below
Outputs:
- filtered: bfloat16 [16, 7168, 2560], P('band', 'lon')
The draws below stay inside these ranges and needn't reach their ends.
Inputs may be any that keep to these rules, and one draw needn't show every extreme that they name: `dest_owner`: at most 2 of the intersections of one device name the same destination owner, and exactly 2 in some device. `filter_len`: the first latitude row has half-width 896.
All inputs are finite; a program needn't handle non-finite values.
Results may differ from the reference program's by a relative error of at most 0.005.
Values may be sent and summed in bfloat16 or wider, within the bound.
A program may use at most 128 MiB of HBM per device.

```python
import math
import jax
import jax.numpy as jnp
import numpy as np
from jax import lax

FIELDS_O = 8
FIELDS_A = 40
LEVELS = 64
LON = 7168
TCELLS = 128
AWIN = 128
CAP = 2
TILES_DEV = 16
BLK_DEV = 32
LAT_DEV = 2
OVL_DEV = 96
INTERSECTIONS = 12288
TILES = 2048
BLOCKS = 4096
LAT = 16
LON_DEV = 448
HALF = 896
WINDOWS = 7
CH = 2560
N_BAND = 8
N_LON = 16
DEVICES = 128


def draw_filter_len(key, part):
    lengths = jax.random.randint(key, (LAT,), LON_DEV + 1, HALF + 1, dtype=jnp.int32)
    return lengths.at[0].set(HALF)


def set_ends(entries, key, least, top_value):
    longest = entries.shape.index(max(entries.shape))
    spots = []
    for shift in (0, 1):
        where = [jax.random.randint(jax.random.fold_in(key, axis), (), 0, length) for axis, length in enumerate(entries.shape)]
        where[longest] = (where[longest] + shift) % entries.shape[longest]
        spots.append(tuple(where))
    return entries.at[spots[0]].set(least).at[spots[1]].set(top_value)


def shard_levels(key, shape, cuts, smallest, top_value):
    loudness, own = 1.0, jax.random.fold_in(key, 6)
    for position, parts in cuts:
        steps = jnp.exp(jax.random.uniform(jax.random.fold_in(own, position), (parts,), jnp.float32, smallest / len(cuts), top_value / len(cuts)))
        loudness = loudness * jnp.repeat(steps, shape[position] // parts).reshape([-1 if axis == position else 1 for axis in range(len(shape))])
    return loudness


def deal_out(rng, own, number, rows, count, top, reach, skew):
    order = jax.random.permutation(rng, count)
    packed, common = shares(count, rows * top, reach, skew, True), shares(count, rows * top, reach, skew, False)
    places = jnp.arange(count)

    def named(sizes, rotation):
        used = int((sizes > 0).sum())
        fixed = max(1, used // 4)
        shifted = fixed + (places - fixed + rotation * (used - fixed)) % max(1, count - fixed)
        return jnp.zeros((count,), jnp.int32).at[order[jnp.where(places < fixed, places, shifted)]].set(jnp.asarray(sizes, jnp.int32))

    sizes = jnp.where(number % 4 == 0, named(packed, number // 4), named(common, number - number // 4 - 1))
    mixed = jax.random.permutation(jax.random.fold_in(own, 3), count)
    source_of, receiver = mixed[0:count // 2 * 2:2], mixed[1:count // 2 * 2:2]
    room = jnp.minimum(sizes[source_of] - 1, reach - sizes[receiver]) // 2
    room = jnp.where((source_of == order[0]) | (receiver == order[0]) | (sizes[receiver] == 0), 0, jnp.maximum(room, 0))
    shifted = jax.random.randint(jax.random.fold_in(own, 4), (count // 2,), 0, 1 << 20) % (room + 1)
    sizes = sizes.at[source_of].add(-shifted).at[receiver].add(shifted)
    labels = jnp.searchsorted(jnp.cumsum(sizes), jnp.arange(rows * top), side="right").astype(jnp.int32)
    table = labels.reshape(top, rows).T
    table = table[jax.random.permutation(jax.random.fold_in(own, 1), rows)]
    rotation = jax.random.randint(jax.random.fold_in(own, 2), (rows, 1), 0, top)
    return jnp.take_along_axis(table, (jnp.arange(top)[None, :] + rotation) % top, axis=1)


def shares(count, total, most, lean, full):
    portions = [(1 << 20) // math.isqrt(standing ** lean) + 1 for standing in range(1, count + 1)]
    largest = most if full else min(most, max(-(-total // count), total * portions[0] // sum(portions)))
    least = 1 if total - largest >= count - 1 else 0
    counts, rest = [largest] + [least] * (count - 1), total - largest - least * (count - 1)
    while rest > 0:
        candidates = [i for i in range(1, count) if counts[i] < largest] or [i for i in range(1, count) if counts[i] < most]
        mass, left = sum([portions[i] for i in candidates]), rest
        for i in candidates:
            addition = min(most - counts[i], max(1, left * portions[i] // mass), rest)
            counts[i] = counts[i] + addition
            rest = rest - addition
    return np.array(counts)


def bell_draw(key, shape, width, reach, shards=(), kind=jnp.bfloat16):
    array = width * jax.random.normal(key, shape, jnp.float32)
    if shards:
        array = array * shard_levels(key, shape, shards, -0.22, 0.18)
    return jnp.clip(array, -reach, reach).astype(kind)


def setup_inputs(seed: int = 0) -> dict:
    key_of = jax.random.split(jax.random.key(seed), 10)
    ocean_flux = bell_draw(key_of[0], (TILES, FIELDS_O, TCELLS), 1.0, 6.0, ((0, 128),))
    remap_weight = bell_draw(key_of[1], (BLOCKS, TCELLS, AWIN), TCELLS ** -0.5, 0.5, ((0, 128),))
    dest_owner_keys = jax.random.split(jax.random.fold_in(key_of[2], 1), INTERSECTIONS // OVL_DEV)
    dest_owner_turns = jax.random.permutation(jax.random.fold_in(key_of[2], 3), INTERSECTIONS // OVL_DEV)
    dest_owner = jax.vmap(lambda own, number: deal_out(jax.random.fold_in(key_of[2], 2), own, number, OVL_DEV, DEVICES, 1, CAP, 2))(dest_owner_keys, dest_owner_turns).reshape((INTERSECTIONS, 1))
    src_tile = set_ends(jax.random.randint(key_of[3], (INTERSECTIONS,), 0, TILES_DEV), jax.random.fold_in(key_of[3], 1), 0, TILES_DEV - 1).astype(jnp.int32)
    weight_block = set_ends(jax.random.randint(key_of[4], (INTERSECTIONS,), 0, BLK_DEV), jax.random.fold_in(key_of[4], 1), 0, BLK_DEV - 1).astype(jnp.int32)
    dest_window = set_ends(jax.random.randint(key_of[5], (INTERSECTIONS,), 0, WINDOWS), jax.random.fold_in(key_of[5], 1), 0, WINDOWS - 1).astype(jnp.int32)
    atmos_state = bell_draw(key_of[6], (LAT, LON, CH), 1.0, 6.0, ((0, 8), (1, 16)))
    profile = jnp.clip(jnp.exp(math.log(3.0) - 2.3025851 * jax.random.uniform(key_of[7], (LAT, HALF + 1), jnp.float32) ** shard_levels(key_of[7], (LAT, HALF + 1), ((0, 8),), -0.2, 0.2)), 0.3, 3.0)
    filter_len = draw_filter_len(jax.random.fold_in(key_of[9], 71), 0)
    return dict(ocean_flux=ocean_flux, remap_weight=remap_weight, dest_owner=dest_owner, src_tile=src_tile, weight_block=weight_block, dest_window=dest_window, atmos_state=atmos_state, profile=profile, filter_len=filter_len)


def make_kernel(profile_row, length):
    half = profile_row.shape[0] - 1
    taps = jnp.concatenate([profile_row[::-1], profile_row[1:]])
    distance = jnp.abs(jnp.arange(2 * half + 1, dtype=jnp.int32) - half)
    taps = jnp.where(distance <= length, taps, jnp.zeros_like(taps))
    return (taps / jnp.sqrt(jnp.sum(taps * taps))).astype(jnp.bfloat16)

def reference(ocean_flux, remap_weight, dest_owner, src_tile, weight_block, dest_window, atmos_state, profile, filter_len):
    owners = dest_owner[:, 0]

    def one_source(total, source):
        start = source * OVL_DEV
        dests = lax.dynamic_slice_in_dim(owners, start, OVL_DEV)
        tile_ids = lax.dynamic_slice_in_dim(src_tile, start, OVL_DEV)
        block_ids = lax.dynamic_slice_in_dim(weight_block, start, OVL_DEV)
        window_ids = lax.dynamic_slice_in_dim(dest_window, start, OVL_DEV)
        tile_rows = lax.dynamic_slice_in_dim(ocean_flux, source * TILES_DEV, TILES_DEV)[tile_ids]
        blocks = lax.dynamic_slice_in_dim(remap_weight, source * BLK_DEV, BLK_DEV)[block_ids]
        contrib = jnp.einsum('ofc,oca->ofa', tile_rows.astype(jnp.float32), blocks.astype(jnp.float32))
        segment = dests * WINDOWS + window_ids
        return (total + jax.ops.segment_sum(contrib, segment, num_segments=DEVICES * WINDOWS), None)
    window_flux, _ = lax.scan(one_source, jnp.zeros((DEVICES * WINDOWS, FIELDS_O, AWIN), jnp.float32), jnp.arange(DEVICES, dtype=jnp.int32))
    flux = window_flux.reshape(N_BAND, N_LON, WINDOWS, FIELDS_O, AWIN).transpose(0, 1, 3, 2, 4)
    flux = flux.reshape(N_BAND, N_LON, FIELDS_O, LAT_DEV, LON_DEV).transpose(0, 3, 1, 4, 2).reshape(LAT, LON, FIELDS_O)
    grid = atmos_state.reshape(LAT, LON, FIELDS_A, LEVELS)
    lowest = (grid[:, :, :FIELDS_O, 0].astype(jnp.float32) + flux).astype(jnp.bfloat16)
    forced = grid.at[:, :, :FIELDS_O, 0].set(lowest).reshape(LAT, LON, CH)
    kernels = jax.vmap(make_kernel)(profile, filter_len)
    offsets = (jnp.arange(2 * HALF + 1, dtype=jnp.int32) - HALF) % LON

    def filter_row(pair):
        row, kernel = pair
        wrapped = jnp.zeros((LON,), jnp.float32).at[offsets].set(kernel.astype(jnp.float32))
        spectrum = jnp.conj(jnp.fft.rfft(wrapped))
        result = jnp.fft.irfft(jnp.fft.rfft(row.astype(jnp.float32), axis=0) * spectrum[:, None], n=LON, axis=0)
        return result.astype(jnp.bfloat16)
    return lax.map(filter_row, (forced, kernels))
```

```python
import jax
import jax.numpy as jnp
from jax import lax
from jax.sharding import PartitionSpec as P

FIELDS_O = 8
FIELDS_A = 40
LEVELS = 64
AWIN = 128
CAP = 2
GROUP = 4
HIGHEST = lax.Precision.HIGHEST


def xor_pairs(count, k):
    return [(source, source ^ k) for source in range(count)]


def shift_pairs(count, steps):
    return [(source, (source + steps) % count) for source in range(count)]


def make_kernel(profile_row, length):
    half = profile_row.shape[0] - 1
    taps = jnp.concatenate([profile_row[::-1], profile_row[1:]])
    distance = jnp.abs(jnp.arange(2 * half + 1, dtype=jnp.int32) - half)
    taps = jnp.where(distance <= length, taps, jnp.zeros_like(taps))
    return (taps / jnp.sqrt(jnp.sum(taps * taps))).astype(jnp.bfloat16)


def band_matrix(profile_row, length, lon_dev):
    kernel = make_kernel(profile_row, length)
    padded = jnp.concatenate([kernel, jnp.zeros((lon_dev,), jnp.bfloat16)])
    width = padded.shape[0] - 1
    return jnp.tile(padded, lon_dev)[: lon_dev * width].reshape(lon_dev, width)


def remap_delta(ocean_flux, remap_weight, dest_owner, src_tile, weight_block, dest_window,
                atmos_state, owners_total):
    lat_dev, lon_dev, _ = atmos_state.shape
    windows = lat_dev * lon_dev // AWIN
    n_tile, n_block = ocean_flux.shape[0], remap_weight.shape[0]
    n_slot = owners_total * CAP
    owners = dest_owner[:, 0]
    pairs = jnp.einsum("tfc,bca->tbfa", ocean_flux, remap_weight,
                       preferred_element_type=jnp.float32)
    pairs = pairs.reshape(n_tile * n_block, FIELDS_O * AWIN)
    contrib = jnp.take(pairs, src_tile * n_block + weight_block, axis=0)
    matches = (owners[:, None] == jnp.arange(owners_total, dtype=jnp.int32)[None, :]).astype(jnp.int32)
    slot_rank = jnp.sum((jnp.cumsum(matches, axis=0) - matches) * matches, axis=1)
    slot_index = owners * CAP + slot_rank
    slot_hot = (slot_index[:, None] == jnp.arange(n_slot, dtype=jnp.int32)[None, :]).astype(jnp.float32)
    outgoing = jnp.einsum("os,oc->sc", slot_hot, contrib, precision=HIGHEST)
    win = jnp.einsum("os,o->s", slot_hot, dest_window.astype(jnp.float32), precision=HIGHEST)
    payload = jnp.concatenate([outgoing, jnp.broadcast_to(win[:, None], (n_slot, AWIN))], axis=1)
    received = lax.all_to_all(payload, ("band", "lon"), 0, 0, tiled=True)
    recv_win = received[:, FIELDS_O * AWIN]
    selector = (recv_win[None, :] == jnp.arange(windows, dtype=jnp.float32)[:, None]).astype(jnp.float32)
    window_flux = jnp.dot(selector, received[:, : FIELDS_O * AWIN], precision=HIGHEST)
    flux = window_flux.reshape(windows, FIELDS_O, AWIN).transpose(1, 0, 2)
    flux = flux.reshape(FIELDS_O, lat_dev, lon_dev).transpose(1, 0, 2)
    raw = atmos_state[:, :, : FIELDS_O * LEVELS : LEVELS].transpose(0, 2, 1).astype(jnp.float32)
    forced = (raw + flux).astype(jnp.bfloat16).astype(jnp.float32)
    return forced - raw


def on_device(
    ocean_flux,
    remap_weight,
    dest_owner,
    src_tile,
    weight_block,
    dest_window,
    atmos_state,
    profile,
    filter_len,
):
    n_band = lax.axis_size("band")
    n_lon = lax.axis_size("lon")
    lat_dev, lon_dev, ch = atmos_state.shape
    half = profile.shape[1] - 1
    cs = ch // GROUP
    span = GROUP * lon_dev
    width = lon_dev + 2 * half
    assert n_lon % GROUP == 0 and ch % GROUP == 0 and half <= span

    j = lax.axis_index("lon")
    r = j % GROUP
    z = j // GROUP
    n_group = n_lon // GROUP

    delta = remap_delta(ocean_flux, remap_weight, dest_owner, src_tile, weight_block,
                        dest_window, atmos_state, n_band * n_lon)
    delta_all = lax.all_gather(delta, "lon", axis=0)
    blocks = 2 * half // lon_dev + GROUP
    first = (z * GROUP - half // lon_dev) % n_lon
    delta_win = lax.dynamic_slice_in_dim(
        jnp.concatenate([delta_all, delta_all], axis=0), first, blocks, axis=0)
    global_ch = r * cs + jnp.arange(cs, dtype=jnp.int32)
    field_of = global_ch // LEVELS
    is_forced = (global_ch % LEVELS == 0) & (field_of < FIELDS_O)

    results = []
    for t in range(lat_dev):
        matrix = band_matrix(profile[t], filter_len[t], lon_dev)
        x_t = atmos_state[t]
        group = jnp.zeros((span, cs), atmos_state.dtype)
        for k in range(GROUP):
            part = lax.dynamic_slice_in_dim(x_t, (r ^ k) * cs, cs, axis=1)
            if k:
                part = lax.ppermute(part, "lon", xor_pairs(n_lon, k))
            group = lax.dynamic_update_slice_in_dim(group, part, (r ^ k) * lon_dev, axis=0)
        west = lax.ppermute(group[span - half:], "lon", shift_pairs(n_lon, GROUP))
        east = lax.ppermute(group[:half], "lon", shift_pairs(n_lon, -GROUP))
        segments = ((0, west), (half, group), (half + span, east))
        d_t = delta_win[:, t].transpose(1, 0, 2).reshape(FIELDS_O, blocks * lon_dev)
        outs = []
        for q in range(GROUP):
            start = q * lon_dev
            acc = None
            for seg_start, seg in segments:
                a = max(start, seg_start)
                b = min(start + width, seg_start + seg.shape[0])
                if a >= b:
                    continue
                term = jnp.dot(matrix[:, a - start : b - start], seg[a - seg_start : b - seg_start],
                               preferred_element_type=jnp.float32)
                acc = term if acc is None else acc + term
            corr = jnp.einsum("fc,ic->if", d_t[:, start : start + width],
                              matrix.astype(jnp.float32), precision=HIGHEST)
            extra = jnp.zeros_like(acc)
            for f in range(FIELDS_O):
                extra = extra + jnp.where(is_forced & (field_of == f), corr[:, f : f + 1], 0.0)
            outs.append((acc + extra).astype(jnp.bfloat16))
        out_t = jnp.concatenate(outs, axis=0)
        final = jnp.zeros((lon_dev, ch), atmos_state.dtype)
        for k in range(GROUP):
            part = lax.dynamic_slice_in_dim(out_t, (r ^ k) * lon_dev, lon_dev, axis=0)
            if k:
                part = lax.ppermute(part, "lon", xor_pairs(n_lon, k))
            final = lax.dynamic_update_slice_in_dim(final, part, (r ^ k) * cs, axis=1)
        results.append(final)
    del n_group
    return jnp.stack(results, axis=0)


def solution(mesh):
    in_specs = (
        P(("band", "lon"), None, None),
        P(("band", "lon"), None, None),
        P(("band", "lon"), None),
        P(("band", "lon")),
        P(("band", "lon")),
        P(("band", "lon")),
        P("band", "lon", None),
        P("band", None),
        P("band"),
    )
    out_specs = P("band", "lon", None)
    return jax.shard_map(
        on_device, mesh=mesh, in_specs=in_specs, out_specs=out_specs, check_vma=False
    )
```

```python
import jax
import jax.numpy as jnp
from jax import lax
from jax.sharding import PartitionSpec as P

FIELDS_O = 8
FIELDS_A = 40
LEVELS = 64
AWIN = 128
CAP = 2
GROUP = 4
HIGHEST = lax.Precision.HIGHEST


def xor_pairs(count, k):
    return [(source, source ^ k) for source in range(count)]


def shift_pairs(count, steps):
    return [(source, (source + steps) % count) for source in range(count)]


def make_kernel(profile_row, length):
    half = profile_row.shape[0] - 1
    taps = jnp.concatenate([profile_row[::-1], profile_row[1:]])
    distance = jnp.abs(jnp.arange(2 * half + 1, dtype=jnp.int32) - half)
    taps = jnp.where(distance <= length, taps, jnp.zeros_like(taps))
    return (taps / jnp.sqrt(jnp.sum(taps * taps))).astype(jnp.bfloat16)


def band_matrix(profile_row, length, lon_dev):
    kernel = make_kernel(profile_row, length)
    padded = jnp.concatenate([kernel, jnp.zeros((lon_dev,), jnp.bfloat16)])
    width = padded.shape[0] - 1
    return jnp.tile(padded, lon_dev)[: lon_dev * width].reshape(lon_dev, width)


def remap_forced(ocean_flux, remap_weight, dest_owner, src_tile, weight_block, dest_window,
                 atmos_state, owners_total):
    lat_dev, lon_dev, _ = atmos_state.shape
    windows = lat_dev * lon_dev // AWIN
    n_tile, n_block = ocean_flux.shape[0], remap_weight.shape[0]
    n_slot = owners_total * CAP
    owners = dest_owner[:, 0]
    pairs = jnp.einsum("tfc,bca->tbfa", ocean_flux, remap_weight,
                       preferred_element_type=jnp.float32)
    pairs = pairs.reshape(n_tile * n_block, FIELDS_O * AWIN)
    contrib = jnp.take(pairs, src_tile * n_block + weight_block, axis=0)
    matches = (owners[:, None] == jnp.arange(owners_total, dtype=jnp.int32)[None, :]).astype(jnp.int32)
    slot_rank = jnp.sum((jnp.cumsum(matches, axis=0) - matches) * matches, axis=1)
    slot_index = owners * CAP + slot_rank
    slot_hot = (slot_index[:, None] == jnp.arange(n_slot, dtype=jnp.int32)[None, :]).astype(jnp.float32)
    outgoing = jnp.einsum("os,oc->sc", slot_hot, contrib, precision=HIGHEST)
    win = jnp.einsum("os,o->s", slot_hot, dest_window.astype(jnp.float32), precision=HIGHEST)
    payload = jnp.concatenate([outgoing, jnp.broadcast_to(win[:, None], (n_slot, AWIN))], axis=1)
    received = lax.all_to_all(payload, ("band", "lon"), 0, 0, tiled=True)
    recv_win = received[:, FIELDS_O * AWIN]
    selector = (recv_win[None, :] == jnp.arange(windows, dtype=jnp.float32)[:, None]).astype(jnp.float32)
    window_flux = jnp.dot(selector, received[:, : FIELDS_O * AWIN], precision=HIGHEST)
    flux = window_flux.reshape(windows, FIELDS_O, AWIN).transpose(1, 0, 2)
    flux = flux.reshape(FIELDS_O, lat_dev, lon_dev).transpose(1, 0, 2)
    raw = atmos_state[:, :, : FIELDS_O * LEVELS : LEVELS].transpose(0, 2, 1).astype(jnp.float32)
    return (raw + flux).astype(jnp.bfloat16)


def on_device(
    ocean_flux,
    remap_weight,
    dest_owner,
    src_tile,
    weight_block,
    dest_window,
    atmos_state,
    profile,
    filter_len,
):
    n_band = lax.axis_size("band")
    n_lon = lax.axis_size("lon")
    lat_dev, lon_dev, ch = atmos_state.shape
    half = profile.shape[1] - 1
    cs = ch // GROUP
    span = GROUP * lon_dev
    width = lon_dev + 2 * half
    assert n_lon % GROUP == 0 and ch % GROUP == 0 and half <= span
    assert (FIELDS_O - 1) * LEVELS < cs and half % lon_dev == 0

    j = lax.axis_index("lon")
    r = j % GROUP
    z = j // GROUP

    forced = remap_forced(ocean_flux, remap_weight, dest_owner, src_tile, weight_block,
                          dest_window, atmos_state, n_band * n_lon)
    reach = half // lon_dev
    near = [lax.ppermute(forced, "lon", shift_pairs(n_lon, -d)) if d else forced
            for d in range(-reach, reach + 1)]
    forced_win = jnp.concatenate(near, axis=2)
    local_ch = jnp.arange(cs, dtype=jnp.int32)
    field_of = local_ch // LEVELS
    is_forced = (local_ch % LEVELS == 0) & (field_of < FIELDS_O)

    results = []
    for t in range(lat_dev):
        matrix = band_matrix(profile[t], filter_len[t], lon_dev)
        x_t = atmos_state[t]
        group = jnp.zeros((span, cs), atmos_state.dtype)
        for k in range(GROUP):
            part = lax.dynamic_slice_in_dim(x_t, (r ^ k) * cs, cs, axis=1)
            if k:
                part = lax.ppermute(part, "lon", xor_pairs(n_lon, k))
            group = lax.dynamic_update_slice_in_dim(group, part, (r ^ k) * lon_dev, axis=0)
        west = lax.ppermute(group[span - half:], "lon", shift_pairs(n_lon, GROUP))
        east = lax.ppermute(group[:half], "lon", shift_pairs(n_lon, -GROUP))
        segments = ((0, west), (half, group), (half + span, east))
        own8 = jnp.einsum("fc,ic->if", forced_win[t], matrix,
                          preferred_element_type=jnp.float32).astype(jnp.bfloat16)
        patch = jnp.zeros((lon_dev, cs), jnp.bfloat16)
        for f in range(FIELDS_O):
            patch = jnp.where(field_of == f, own8[:, f : f + 1], patch)
        outs = []
        for q in range(GROUP):
            start = q * lon_dev
            acc = None
            for seg_start, seg in segments:
                a = max(start, seg_start)
                b = min(start + width, seg_start + seg.shape[0])
                if a >= b:
                    continue
                term = jnp.dot(matrix[:, a - start : b - start], seg[a - seg_start : b - seg_start],
                               preferred_element_type=jnp.float32)
                acc = term if acc is None else acc + term
            outs.append(acc.astype(jnp.bfloat16))
        out_t = jnp.concatenate(outs, axis=0)
        final = jnp.zeros((lon_dev, ch), atmos_state.dtype)
        for k in range(GROUP):
            part = lax.dynamic_slice_in_dim(out_t, (r ^ k) * lon_dev, lon_dev, axis=0)
            if k:
                part = lax.ppermute(part, "lon", xor_pairs(n_lon, k))
            part = jnp.where(((r ^ k) == 0) & is_forced[None, :], patch, part)
            final = lax.dynamic_update_slice_in_dim(final, part, (r ^ k) * cs, axis=1)
        results.append(final)
    return jnp.stack(results, axis=0)


def solution(mesh):
    in_specs = (
        P(("band", "lon"), None, None),
        P(("band", "lon"), None, None),
        P(("band", "lon"), None),
        P(("band", "lon")),
        P(("band", "lon")),
        P(("band", "lon")),
        P("band", "lon", None),
        P("band", None),
        P("band"),
    )
    out_specs = P("band", "lon", None)
    return jax.shard_map(
        on_device, mesh=mesh, in_specs=in_specs, out_specs=out_specs, check_vma=False
    )
```
